32 devices in a mesh: replica: 16 (over z, y, core), tp: 2 (over x).
Axes of the slice: x: 2, y: 2, z: 4, core: 2. Of those that a mesh axis runs over, the one named last changes fastest.
Arguments:
- states: bfloat16 [8, 256, 4608], P(None, 'replica'), may hold values from -6 to 6
- pre_gain: float32 [4608], replicated, may hold values from 0.5 to 1.5
- post_gain: float32 [4608], replicated, may hold values from 0.5 to 1.5
- query_weight: bfloat16 [4608, 2048], P(None, 'tp'), may hold values from -0.09375 to 0.09375
- key_weight: bfloat16 [4608, 1024], P(None, 'tp'), may hold values from -0.09375 to 0.09375
- value_weight: bfloat16 [4608, 1024], P(None, 'tp'), may hold values from -0.09375 to 0.09375
- out_weight: bfloat16 [2048, 4608], P('tp')
- cache_keys: bfloat16 [4096, 16, 1024], P('replica', None, 'tp'), may hold values from -6 to 6
- cache_values: bfloat16 [4096, 16, 1024], P('replica', None, 'tp'), may hold values from -6 to 6
- context: int32 [256], replicated, may hold values from 1 to 248
- slot_map: int32 [8, 256], replicated, may hold values from 0 to 255, each once within a row
Outputs:
- decoded: bfloat16 [8, 256, 4608], P(None, 'replica')
- moved_keys: bfloat16 [4096, 16, 1024], P('replica', None, 'tp')
- moved_values: bfloat16 [4096, 16, 1024], P('replica', None, 'tp')
The draws below stay inside these ranges and needn't reach their ends.
Inputs may be any that keep to these rules, and one draw needn't show every extreme that they name: `slot_map`: each row names every page of one replica set once.
All inputs are finite; a program needn't handle non-finite values.
Results may differ from the reference program's by a relative error of at most 0.012.
Values may be sent and summed in bfloat16 or wider, within the bound.
A program may use at most 128 MiB of HBM per device.

```python
import math
import jax
import jax.numpy as jnp
from jax import lax

D = 4608
H = 16
KVH = 8
HD = 128
PAGE = 16
STEPS = 8
B = 16
PPR = 16
REPLICAS = 16
PAIRS = 8
N_REPLICA = 16
N_TP = 2


def draw_out_weight(key, part):
    first_key, second_key = jax.random.split(key, 2)
    base = jax.random.normal(first_key, (H * HD, D), jnp.float32) / jnp.sqrt(jnp.float32(H * HD))
    ramp = jnp.arange(D, dtype=jnp.float32) / D
    rough = jnp.exp(jax.random.uniform(second_key, (D,), jnp.float32, jnp.log(0.5), jnp.log(2.0)))
    column_scale = jnp.exp(jnp.log(3.0) * ramp) * rough
    return (base * column_scale[None, :]).astype(jnp.bfloat16)


def touch_ends(entries, rng, low, top_value):
    extent = entries.shape
    spot = [jax.random.randint(jax.random.fold_in(rng, axis), (), 0, extent[axis]) for axis in range(len(extent))]
    entries = entries.at[tuple(spot)].set(low)
    longest = extent.index(max(extent))
    spot[longest] = (spot[longest] + 1) % extent[longest]
    return entries.at[tuple(spot)].set(top_value)


def block_scale(own_key, shape, cuts, least, largest):
    factor_of, own = 1.0, jax.random.fold_in(own_key, 6)
    for position, blocks in cuts:
        heights = jnp.exp(jax.random.uniform(jax.random.fold_in(own, position), (blocks,), jnp.float32, least / len(cuts), largest / len(cuts)))
        factor_of = factor_of * jnp.repeat(heights, shape[position] // blocks).reshape([-1 if axis == position else 1 for axis in range(len(shape))])
    return factor_of


def bell_draw(key, dims, scale, limit, cuts=(), kind=jnp.bfloat16):
    entries = scale * jax.random.normal(key, dims, jnp.float32)
    if cuts:
        entries = entries * block_scale(key, dims, cuts, -0.22, 0.18)
    return jnp.clip(entries, -limit, limit).astype(kind)


def setup_inputs(seed: int = 0) -> dict:
    key_of = jax.random.split(jax.random.key(seed), 12)
    states = bell_draw(key_of[0], (STEPS, REPLICAS * B, D), 1.0, 6.0, ((1, 16),))
    pre_gain = jnp.clip(1.0 + 0.1 * jax.random.normal(key_of[1], (D,), jnp.float32), 0.5, 1.5)
    post_gain = jnp.clip(1.0 + 0.1 * jax.random.normal(key_of[2], (D,), jnp.float32), 0.5, 1.5)
    query_weight = bell_draw(key_of[3], (D, H * HD), D ** -0.5, 0.09375, ((1, 2),))
    key_weight = bell_draw(key_of[4], (D, KVH * HD), D ** -0.5, 0.09375, ((1, 2),))
    value_weight = bell_draw(key_of[5], (D, KVH * HD), D ** -0.5, 0.09375, ((1, 2),))
    out_weight = draw_out_weight(jax.random.fold_in(key_of[11], 71), 0)
    cache_keys = bell_draw(key_of[7], (REPLICAS * B * PPR, PAGE, KVH * HD), 1.0, 6.0, ((0, 16), (2, 2)))
    cache_values = bell_draw(key_of[8], (REPLICAS * B * PPR, PAGE, KVH * HD), 1.0, 6.0, ((0, 16), (2, 2)))
    context = touch_ends(jax.random.randint(key_of[9], (REPLICAS * B,), 1, PPR * PAGE - STEPS + 1), jax.random.fold_in(key_of[9], 1), 1, PPR * PAGE - STEPS).astype(jnp.int32)
    slot_map = jax.vmap(lambda own: jax.random.permutation(own, B * PPR))(jax.random.split(key_of[10], PAIRS)).reshape((PAIRS, B * PPR)).astype(jnp.int32)
    return dict(states=states, pre_gain=pre_gain, post_gain=post_gain, query_weight=query_weight, key_weight=key_weight, value_weight=value_weight, out_weight=out_weight, cache_keys=cache_keys, cache_values=cache_values, context=context, slot_map=slot_map)


epsilon = 1e-06
softcap = 50.0
query_scalar = 144.0

def rotate(vectors, positions):
    halfway = vectors.shape[-1] // 2
    frequency = 10000.0 ** (-jnp.arange(halfway, dtype=jnp.float32) / halfway)
    angles = (positions.astype(jnp.float32)[:, None] * frequency[None, :])[:, None, :]
    cosine = jnp.cos(angles)
    sines = jnp.sin(angles)
    leading = vectors[..., :halfway]
    trailing = vectors[..., halfway:]
    return jnp.concatenate([leading * cosine - trailing * sines, trailing * cosine + leading * sines], axis=-1)

def place_pages(slot_ids, source_pages):
    return jnp.zeros_like(source_pages).at[slot_ids].set(source_pages)

def reference(states, pre_gain, post_gain, query_weight, key_weight, value_weight, out_weight, cache_keys, cache_values, context, slot_map):
    requests = N_REPLICA * B
    length = PPR * PAGE
    kv_width = KVH * HD
    group_size = H // KVH
    keys_flat = cache_keys.reshape(requests * length, kv_width)
    values_flat = cache_values.reshape(requests * length, kv_width)
    offsets = jnp.arange(requests, dtype=jnp.int32) * length
    position_grid = jnp.arange(length, dtype=jnp.int32)
    out_groups = out_weight.reshape(N_TP, H * HD // N_TP, D).astype(jnp.float32)
    outputs = []
    for index in range(STEPS):
        current = states[index].astype(jnp.float32)
        normed = (current * lax.rsqrt(lax.optimization_barrier(jnp.mean(current * current, axis=-1, keepdims=True)) + epsilon) * pre_gain).astype(jnp.bfloat16)
        queries = jnp.dot(normed, query_weight, preferred_element_type=jnp.float32).reshape(requests, H, HD)
        new_keys = jnp.dot(normed, key_weight, preferred_element_type=jnp.float32).reshape(requests, KVH, HD)
        new_values = jnp.dot(normed, value_weight, preferred_element_type=jnp.float32).astype(jnp.bfloat16)
        positions = context + index
        queries = rotate(queries, positions).astype(jnp.bfloat16).reshape(requests, KVH, group_size, HD)
        new_keys = rotate(new_keys, positions).astype(jnp.bfloat16).reshape(requests, kv_width)
        rows = offsets + positions
        keys_flat = keys_flat.at[rows].set(new_keys)
        values_flat = values_flat.at[rows].set(new_values)
        key_view = keys_flat.reshape(requests, length, KVH, HD).astype(jnp.float32)
        value_view = values_flat.reshape(requests, length, KVH, HD).astype(jnp.float32)
        scores = jnp.einsum('rkgd,rlkd->rkgl', queries.astype(jnp.float32), key_view)
        scores = softcap * jnp.tanh(scores / (softcap * math.sqrt(query_scalar)))
        visible = position_grid[None, None, None, :] <= positions[:, None, None, None]
        expo = jnp.where(visible, jnp.exp(scores), 0.0)
        attn_weights = (expo / lax.optimization_barrier(jnp.sum(expo, axis=-1, keepdims=True))).astype(jnp.bfloat16)
        attended = jnp.einsum('rkgl,rlkd->rkgd', attn_weights.astype(jnp.float32), value_view).astype(jnp.bfloat16)
        attended = attended.reshape(requests, N_TP, H * HD // N_TP).astype(jnp.float32)
        partials = jnp.einsum('rgc,gcd->grd', attended, out_groups)
        rounded = lax.optimization_barrier(partials.astype(jnp.bfloat16))
        summed = lax.optimization_barrier(jnp.sum(rounded.astype(jnp.float32), axis=0))
        inverse = lax.rsqrt(lax.optimization_barrier(jnp.mean(summed * summed, axis=-1, keepdims=True)) + epsilon)
        outputs.append((current + summed * inverse * post_gain).astype(jnp.bfloat16))
    decoded = jnp.stack(outputs)
    final_keys = keys_flat.reshape(N_REPLICA, B * PPR, PAGE, kv_width)
    final_values = values_flat.reshape(N_REPLICA, B * PPR, PAGE, kv_width)
    placed_keys = jax.vmap(place_pages)(slot_map, final_keys[:PAIRS])
    placed_values = jax.vmap(place_pages)(slot_map, final_values[:PAIRS])
    moved_keys = jnp.concatenate([final_keys[:PAIRS], placed_keys], axis=0).reshape(N_REPLICA * B * PPR, PAGE, kv_width)
    moved_values = jnp.concatenate([final_values[:PAIRS], placed_values], axis=0).reshape(N_REPLICA * B * PPR, PAGE, kv_width)
    return (decoded, moved_keys, moved_values)
```

```python
import functools
import math

import jax
import jax.numpy as jnp
from jax import lax
from jax.experimental import pallas as pl
from jax.experimental.pallas import tpu as pltpu
from jax.sharding import PartitionSpec as P

HD = 128


epsilon = 1e-06
softcap = 50.0
query_scalar = 144.0


def shifted(value, axis, steps):
    count = lax.axis_size(axis)
    initial, last = (max(0, -steps), min(count, count - steps))
    return lax.ppermute(value, axis, [(source, source + steps) for source in range(initial, last)])


def rotate(vectors, positions):
    halfway = vectors.shape[-1] // 2
    frequency = 10000.0 ** (-jnp.arange(halfway, dtype=jnp.float32) / halfway)
    angles = (positions.astype(jnp.float32)[:, None] * frequency[None, :])[:, None, :]
    cosine = jnp.cos(angles)
    sines = jnp.sin(angles)
    leading = vectors[..., :halfway]
    trailing = vectors[..., halfway:]
    return jnp.concatenate(
        [leading * cosine - trailing * sines, trailing * cosine + leading * sines], axis=-1
    )


def write_rows(cache, rows, lengths):
    grid = jnp.arange(cache.shape[1], dtype=jnp.int32)[None, :] - lengths[:, None]
    for step in range(rows.shape[1]):
        cache = jnp.where((grid == step)[:, :, None], rows[:, step][:, None, :], cache)
    return cache


def place_kernel(pages, group, slots, flag, own, received, *rest):
    out, held, in_sem, out_sem = rest[-4:]
    groups = [(low, min(group, pages - low)) for low in range(0, pages, group)]

    def load(source):
        for index, (low, count) in enumerate(groups):
            pltpu.make_async_copy(
                source.at[pl.ds(low, count)], held.at[pl.ds(low, count)], in_sem.at[index]
            ).start()

    @pl.when(flag[0] != 0)
    def _():
        load(received)

    @pl.when(flag[0] == 0)
    def _():
        load(own)

    for index, (low, count) in enumerate(groups):
        pltpu.make_async_copy(
            own.at[pl.ds(low, count)], held.at[pl.ds(low, count)], in_sem.at[index]
        ).wait()

        def send(page, carry):
            pltpu.make_async_copy(held.at[page], out.at[slots[page]], out_sem).start()
            return carry

        lax.fori_loop(low, low + count, send, 0, unroll=8)
    pltpu.make_async_copy(held, held, out_sem).wait()


def place(region, slots, flag, own, received, total):
    pages = own.shape[0]
    group = 16
    anywhere = pl.BlockSpec(memory_space=pltpu.MemorySpace.HBM)
    scalar = pl.BlockSpec(memory_space=pltpu.SMEM)
    operands = (slots, flag, own, received) + (() if region is None else (region,))
    return pl.pallas_call(
        functools.partial(place_kernel, pages, group),
        out_shape=jax.ShapeDtypeStruct((total,) + own.shape[1:], own.dtype),
        in_specs=[scalar, scalar] + [anywhere] * (len(operands) - 2),
        out_specs=anywhere,
        scratch_shapes=[
            pltpu.VMEM(own.shape, own.dtype),
            pltpu.SemaphoreType.DMA((-(-pages // group),)),
            pltpu.SemaphoreType.DMA,
        ],
        input_output_aliases={} if region is None else {4: 0},
        cost_estimate=pl.CostEstimate(
            flops=0, bytes_accessed=2 * own.size * 2, transcendentals=0
        ),
    )(*operands)


def shards(
    states,
    pre_gain,
    post_gain,
    query_weight,
    key_weight,
    value_weight,
    out_weight,
    cache_keys,
    cache_values,
    context,
    slot_map,
):
    half_count = lax.axis_size("replica") // 2
    tp_count = lax.axis_size("tp")
    replica = lax.axis_index("replica")
    partner = replica % half_count
    steps, requests, model_width = states.shape
    page_count, page_len, kv_width = cache_keys.shape
    per_request = page_count // requests
    length = per_request * page_len
    kv_local = kv_width // HD
    q_local = query_weight.shape[1] // HD
    group_size = q_local // kv_local
    own_lengths = lax.dynamic_slice_in_dim(context, replica * requests, requests)
    pair_lengths = lax.dynamic_slice_in_dim(context, partner * requests, requests)
    slot_ids = lax.dynamic_index_in_dim(slot_map, partner, 0, keepdims=False)
    is_target = replica >= half_count
    slots = jnp.where(is_target, slot_ids, jnp.arange(page_count, dtype=jnp.int32))
    flag = is_target.astype(jnp.int32).reshape(1)

    def paged(rows):
        return rows.reshape(-1, page_len, kv_width)

    def shift(value):
        return shifted(value, "replica", half_count)

    early = max(1, requests // 8)
    late = max(1, requests // 16)
    cuts = ((0, early), (early, requests - late), (requests - late, requests))
    caches = {
        "v": cache_values.reshape(requests, length, kv_width),
        "k": cache_keys.reshape(requests, length, kv_width),
    }
    early_rows = {name: paged(caches[name][:early]) for name in caches}
    states, caches, early_rows = lax.optimization_barrier((states, caches, early_rows))
    raw = {name: shift(early_rows[name]) for name in caches}

    rows_first = states.transpose(1, 0, 2)
    widened = rows_first.astype(jnp.float32)
    squares = jnp.mean(widened * widened, axis=-1, keepdims=True)
    normed = (
        widened
        * lax.rsqrt(squares + epsilon)
        * pre_gain
    ).astype(jnp.bfloat16).reshape(requests * steps, model_width)
    positions = own_lengths[:, None] + jnp.arange(steps, dtype=jnp.int32)[None, :]
    flat_positions = positions.reshape(-1)

    new = {}
    new["v"] = (
        jnp.dot(normed, value_weight, preferred_element_type=jnp.float32)
        .astype(jnp.bfloat16)
        .reshape(requests, steps, kv_width)
    )
    keys = jnp.dot(normed, key_weight, preferred_element_type=jnp.float32)
    new["k"] = (
        rotate(keys.reshape(-1, kv_local, HD), flat_positions)
        .astype(jnp.bfloat16)
        .reshape(requests, steps, kv_width)
    )
    own = {
        name: [
            write_rows(caches[name][low:high], new[name][low:high], own_lengths[low:high])
            for low, high in cuts
        ]
        for name in caches
    }
    middle = {name: shift(paged(own[name][1])) for name in caches}
    delta = shift(jnp.stack([new["k"][:early], new["v"][:early]]))

    queries = jnp.dot(normed, query_weight, preferred_element_type=jnp.float32)
    queries = (
        rotate(queries.reshape(-1, q_local, HD), flat_positions)
        .astype(jnp.bfloat16)
        .reshape(requests, steps, kv_local, group_size, HD)
    )
    grid = jnp.arange(length, dtype=jnp.int32)
    visible = grid[None, None, :] <= positions[:, :, None]
    outs = []
    for index, (low, high) in enumerate(cuts):
        key_view = own["k"][index].reshape(high - low, length, kv_local, HD)
        value_view = own["v"][index].reshape(high - low, length, kv_local, HD)
        scores = jnp.einsum(
            "rtkgd,rlkd->rktgl", queries[low:high], key_view, preferred_element_type=jnp.float32
        )
        scores = softcap * jnp.tanh(scores / (softcap * math.sqrt(query_scalar)))
        expo = jnp.where(visible[low:high, None, :, None, :], jnp.exp(scores), 0.0)
        weights = (expo / jnp.sum(expo, axis=-1, keepdims=True)).astype(jnp.bfloat16)
        attended = jnp.einsum(
            "rktgl,rlkd->rtkgd", weights, value_view, preferred_element_type=jnp.float32
        )
        outs.append(attended.astype(jnp.bfloat16).reshape((high - low) * steps, q_local * HD))
    attended = jnp.concatenate(outs, axis=0)
    partial_sum = jnp.dot(attended, out_weight, preferred_element_type=jnp.float32).astype(
        jnp.bfloat16
    )
    summed = partial_sum.astype(jnp.float32)
    for offset in range(1, tp_count):
        ring = [(source, (source + offset) % tp_count) for source in range(tp_count)]
        summed = summed + lax.ppermute(partial_sum, "tp", ring).astype(jnp.float32)
    inverse = lax.rsqrt(jnp.mean(summed * summed, axis=-1, keepdims=True) + epsilon)
    moved = (summed * inverse * post_gain).reshape(requests, steps, model_width)
    decoded = (widened + moved).astype(jnp.bfloat16).transpose(1, 0, 2)

    last_k, last_v, decoded = lax.optimization_barrier((own["k"][2], own["v"][2], decoded))
    last = {"v": shift(paged(last_v)), "k": shift(paged(last_k))}

    results = {}
    for name, part in (("v", 1), ("k", 0)):
        first = write_rows(
            raw[name].reshape(early, length, kv_width), delta[part], pair_lengths[:early]
        )
        region = None
        received = (paged(first), middle[name], last[name])
        for index, (low, high) in enumerate(cuts):
            region = place(
                region,
                slots[low * per_request : high * per_request],
                flag,
                paged(own[name][index]),
                received[index],
                page_count,
            )
        results[name] = region
    return (decoded, results["k"], results["v"])


def solution(mesh):
    return jax.shard_map(
        shards,
        mesh=mesh,
        in_specs=(
            P(None, "replica", None),
            P(),
            P(),
            P(None, "tp"),
            P(None, "tp"),
            P(None, "tp"),
            P("tp", None),
            P("replica", None, "tp"),
            P("replica", None, "tp"),
            P(),
            P(),
        ),
        out_specs=(P(None, "replica", None), P("replica", None, "tp"), P("replica", None, "tp")),
        check_vma=False,
    )
```

```python
import functools
import math

import jax
import jax.numpy as jnp
from jax import lax
from jax.experimental import pallas as pl
from jax.experimental.pallas import tpu as pltpu
from jax.sharding import PartitionSpec as P

HD = 128


epsilon = 1e-06
softcap = 50.0
query_scalar = 144.0


def shifted(value, axis, steps):
    count = lax.axis_size(axis)
    initial, last = (max(0, -steps), min(count, count - steps))
    return lax.ppermute(value, axis, [(source, source + steps) for source in range(initial, last)])


def rotate(vectors, positions):
    halfway = vectors.shape[-1] // 2
    frequency = 10000.0 ** (-jnp.arange(halfway, dtype=jnp.float32) / halfway)
    angles = (positions.astype(jnp.float32)[:, None] * frequency[None, :])[:, None, :]
    cosine = jnp.cos(angles)
    sines = jnp.sin(angles)
    leading = vectors[..., :halfway]
    trailing = vectors[..., halfway:]
    return jnp.concatenate(
        [leading * cosine - trailing * sines, trailing * cosine + leading * sines], axis=-1
    )


def write_rows(cache, rows, lengths):
    grid = jnp.arange(cache.shape[1], dtype=jnp.int32)[None, :] - lengths[:, None]
    for step in range(rows.shape[1]):
        cache = jnp.where((grid == step)[:, :, None], rows[:, step][:, None, :], cache)
    return cache


def place_kernel(pages, group, first_page, slots_in, own, received, *rest):
    out, held, slots, slot_sem, in_sem, out_sem = rest[-6:]
    is_target = lax.axis_index("replica") >= lax.axis_size("replica") // 2
    slot_copy = pltpu.make_async_copy(slots_in, slots, slot_sem)
    slot_copy.start()
    groups = [(low, min(group, pages - low)) for low in range(0, pages, group)]

    def load(source):
        for index, (low, count) in enumerate(groups):
            pltpu.make_async_copy(
                source.at[pl.ds(low, count)], held.at[pl.ds(low, count)], in_sem.at[index]
            ).start()

    @pl.when(is_target)
    def _():
        load(received)

    @pl.when(jnp.logical_not(is_target))
    def _():
        load(own)

    slot_copy.wait()
    for index, (low, count) in enumerate(groups):
        pltpu.make_async_copy(
            own.at[pl.ds(low, count)], held.at[pl.ds(low, count)], in_sem.at[index]
        ).wait()

        def send(page, carry):
            pltpu.make_async_copy(held.at[page], out.at[slots[first_page + page]], out_sem).start()
            return carry

        lax.fori_loop(low, low + count, send, 0, unroll=8)
    pltpu.make_async_copy(held, held, out_sem).wait()


def place(region, slots, first_page, own, received, total):
    pages = own.shape[0]
    group = 16
    anywhere = pl.BlockSpec(memory_space=pltpu.MemorySpace.HBM)
    operands = (slots, own, received) + (() if region is None else (region,))
    return pl.pallas_call(
        functools.partial(place_kernel, pages, group, first_page),
        out_shape=jax.ShapeDtypeStruct((total,) + own.shape[1:], own.dtype),
        in_specs=[anywhere] * len(operands),
        out_specs=anywhere,
        scratch_shapes=[
            pltpu.VMEM(own.shape, own.dtype),
            pltpu.SMEM(slots.shape, slots.dtype),
            pltpu.SemaphoreType.DMA,
            pltpu.SemaphoreType.DMA((-(-pages // group),)),
            pltpu.SemaphoreType.DMA,
        ],
        input_output_aliases={} if region is None else {3: 0},
        cost_estimate=pl.CostEstimate(
            flops=0, bytes_accessed=2 * own.size * 2, transcendentals=0
        ),
    )(*operands)


def shards(
    states,
    pre_gain,
    post_gain,
    query_weight,
    key_weight,
    value_weight,
    out_weight,
    cache_keys,
    cache_values,
    context,
    slot_map,
):
    half_count = lax.axis_size("replica") // 2
    tp_count = lax.axis_size("tp")
    replica = lax.axis_index("replica")
    partner = replica % half_count
    steps, requests, model_width = states.shape
    page_count, page_len, kv_width = cache_keys.shape
    per_request = page_count // requests
    length = per_request * page_len
    kv_local = kv_width // HD
    q_local = query_weight.shape[1] // HD
    group_size = q_local // kv_local
    own_lengths = lax.dynamic_slice_in_dim(context, replica * requests, requests)
    pair_lengths = lax.dynamic_slice_in_dim(context, partner * requests, requests)
    slot_ids = lax.dynamic_index_in_dim(slot_map, partner, 0, keepdims=False)
    is_target = replica >= half_count
    slots = jnp.where(is_target, slot_ids, jnp.arange(page_count, dtype=jnp.int32))

    def paged(rows):
        return rows.reshape(-1, page_len, kv_width)

    def shift(value):
        return shifted(value, "replica", half_count)

    early = max(1, requests // 8)
    late = max(1, requests // 16)
    cuts = {
        "v": ((0, early), (early, requests - late), (requests - late, requests)),
        "k": ((0, requests - late), (requests - late, requests)),
    }
    caches = {
        "v": cache_values.reshape(requests, length, kv_width),
        "k": cache_keys.reshape(requests, length, kv_width),
    }
    early_rows = paged(caches["v"][:early])
    early_rows = jnp.where(is_target, jnp.zeros_like(early_rows), early_rows)
    states, caches, early_rows = lax.optimization_barrier((states, caches, early_rows))
    raw = shift(early_rows)

    rows_first = states.transpose(1, 0, 2)
    widened = rows_first.astype(jnp.float32)
    squares = jnp.mean(widened * widened, axis=-1, keepdims=True)
    normed = (
        widened
        * lax.rsqrt(squares + epsilon)
        * pre_gain
    ).astype(jnp.bfloat16).reshape(requests * steps, model_width)
    positions = own_lengths[:, None] + jnp.arange(steps, dtype=jnp.int32)[None, :]
    flat_positions = positions.reshape(-1)

    new = {}
    new["v"] = (
        jnp.dot(normed, value_weight, preferred_element_type=jnp.float32)
        .astype(jnp.bfloat16)
        .reshape(requests, steps, kv_width)
    )
    keys = jnp.dot(normed, key_weight, preferred_element_type=jnp.float32)
    new["k"] = (
        rotate(keys.reshape(-1, kv_local, HD), flat_positions)
        .astype(jnp.bfloat16)
        .reshape(requests, steps, kv_width)
    )
    own = {
        name: [
            write_rows(caches[name][low:high], new[name][low:high], own_lengths[low:high])
            for low, high in cuts[name]
        ]
        for name in caches
    }
    middle = {name: shift(paged(own[name][-2])) for name in caches}
    delta = shift(new["v"][:early])

    queries = jnp.dot(normed, query_weight, preferred_element_type=jnp.float32)
    queries = (
        rotate(queries.reshape(-1, q_local, HD), flat_positions)
        .astype(jnp.bfloat16)
        .reshape(requests, steps, kv_local, group_size, HD)
    )
    grid = jnp.arange(length, dtype=jnp.int32)
    visible = grid[None, None, :] <= positions[:, :, None]
    whole = {name: jnp.concatenate(own[name], axis=0) for name in caches}
    key_view = whole["k"].reshape(requests, length, kv_local, HD)
    value_view = whole["v"].reshape(requests, length, kv_local, HD)
    scores = jnp.einsum(
        "rtkgd,rlkd->rktgl", queries, key_view, preferred_element_type=jnp.float32
    )
    scores = softcap * jnp.tanh(scores / (softcap * math.sqrt(query_scalar)))
    expo = jnp.where(visible[:, None, :, None, :], jnp.exp(scores), 0.0)
    weights = (expo / jnp.sum(expo, axis=-1, keepdims=True)).astype(jnp.bfloat16)
    attended = jnp.einsum(
        "rktgl,rlkd->rtkgd", weights, value_view, preferred_element_type=jnp.float32
    )
    attended = attended.astype(jnp.bfloat16).reshape(requests * steps, q_local * HD)
    partial_sum = jnp.dot(attended, out_weight, preferred_element_type=jnp.float32).astype(
        jnp.bfloat16
    )
    summed = partial_sum.astype(jnp.float32)
    for offset in range(1, tp_count):
        ring = [(source, (source + offset) % tp_count) for source in range(tp_count)]
        summed = summed + lax.ppermute(partial_sum, "tp", ring).astype(jnp.float32)
    inverse = lax.rsqrt(jnp.mean(summed * summed, axis=-1, keepdims=True) + epsilon)
    moved = (summed * inverse * post_gain).reshape(requests, steps, model_width)
    decoded = (widened + moved).astype(jnp.bfloat16).transpose(1, 0, 2)

    last_k, last_v, decoded = lax.optimization_barrier((own["k"][-1], own["v"][-1], decoded))
    last = {"v": shift(paged(last_v)), "k": shift(paged(last_k))}

    first = write_rows(raw.reshape(early, length, kv_width), delta, pair_lengths[:early])
    received = {"v": (paged(first), middle["v"], last["v"]), "k": (middle["k"], last["k"])}

    def fill(region, name, index, chunk):
        low = cuts[name][index][0]
        return place(
            region, slots, low * per_request, paged(own[name][index]), chunk, page_count
        )

    placed_v = fill(None, "v", 0, received["v"][0])
    placed_v = fill(placed_v, "v", 1, received["v"][1])
    placed_v, middle_k = lax.optimization_barrier((placed_v, received["k"][0]))
    placed_k = fill(None, "k", 0, middle_k)
    placed_k, last_v = lax.optimization_barrier((placed_k, received["v"][2]))
    placed_v = fill(placed_v, "v", 2, last_v)
    placed_v, last_k = lax.optimization_barrier((placed_v, received["k"][1]))
    results = {"v": placed_v, "k": fill(placed_k, "k", 1, last_k)}
    return (decoded, results["k"], results["v"])


def solution(mesh):
    return jax.shard_map(
        shards,
        mesh=mesh,
        in_specs=(
            P(None, "replica", None),
            P(),
            P(),
            P(None, "tp"),
            P(None, "tp"),
            P(None, "tp"),
            P("tp", None),
            P("replica", None, "tp"),
            P("replica", None, "tp"),
            P(),
            P(),
        ),
        out_specs=(P(None, "replica", None), P("replica", None, "tp"), P("replica", None, "tp")),
        check_vma=False,
    )
```
